512 devices in a mesh: rep: 16 (over x, z_lo, core), dp: 32 (over y, z_hi).
Axes of the slice: x: 4, y: 8, z: 8 (z_hi: 4, z_lo: 2; z = z_hi * 2 + z_lo), core: 2. Of those that a mesh axis runs over, the one named last changes fastest.
Arguments:
- image_features: bfloat16 [65536, 1408], P(('rep', 'dp')), parts along dimension 0, may hold values from -24 to 24
- text_embed: bfloat16 [65536, 512], P(('rep', 'dp')), parts along dimension 0, may hold values from -24 to 24
- image_head: bfloat16 [22528, 512], P(('rep', 'dp')), parts along dimension 0, may hold values from -1 to 3
- logit_scale: float32 [1], replicated, may hold values from 10 to 40
Outputs:
- image_features_grad: bfloat16 [65536, 1408], P(('rep', 'dp')), parts along dimension 0
- text_embed_grad: bfloat16 [65536, 512], P(('rep', 'dp')), parts along dimension 0
- image_head_grad: float32 [22528, 512], P(('rep', 'dp')), parts along dimension 0
The draws below stay inside these ranges and needn't reach their ends.
There are 16 independent parts, one for each index of `rep`. The reference program is written for one: setup_inputs(seed, part) draws one part's arguments, and reference() takes and returns one part's arrays. A program takes and returns all parts, laid end to end along the dimension named above; an argument that names none is the same for every part. Nothing has to cross between parts.
All inputs are finite; a program needn't handle non-finite values.
Results may differ from the reference program's by a relative error of at most 0.02.
Values may be sent and summed in bfloat16 or wider, within the bound.
No kernel may reach another device: no remote copies, remote signals or barrier semaphores. Data moves between devices by JAX's collectives and lax.ppermute only.
A program may use at most 64 MiB of HBM per device.

```python
import math
import jax
import jax.numpy as jnp
from jax import lax

DI = 1408
E = 512
B = 4096
N_DP = 32


def noise_block(key, shape):
    return jax.random.normal(key, shape, jnp.float32)


def latent_rows(key):
    base = jax.random.fold_in(key, 4101)
    topic_key, center_key, pull_key, own_key = jax.random.split(base, 4)
    topics = max(B // 16, 4)
    topic_ids = jax.random.randint(topic_key, (B,), 0, topics)
    centers = jax.random.normal(center_key, (topics, E), jnp.float32)
    pull = jnp.exp(jax.random.uniform(pull_key, (B, 1), jnp.float32, math.log(0.3), math.log(3.0)))
    return pull * centers[topic_ids] + noise_block(own_key, (B, E))


def draw_text_embed(key, part):
    latent = latent_rows(key)
    values = latent + 0.5 * noise_block(jax.random.fold_in(key, 4102), (B, E))
    return jnp.clip(values, -24.0, 24.0).astype(jnp.bfloat16)


def draw_image_features(key, part):
    latent = latent_rows(key)
    leading = latent + 0.5 * noise_block(jax.random.fold_in(key, 4104), (B, E))
    trailing = noise_block(jax.random.fold_in(key, 4105), (B, DI - E))
    values = jnp.concatenate([leading, trailing], axis=1)
    return jnp.clip(values, -24.0, 24.0).astype(jnp.bfloat16)


def draw_image_head(key, part):
    bound = 4.0 / math.sqrt(DI)
    noise = noise_block(jax.random.fold_in(key, 4107), (DI, E)) / math.sqrt(DI)
    noise = jnp.clip(noise, -bound, bound)
    row_ids = jax.lax.broadcasted_iota(jnp.int32, (DI, E), 0)
    col_ids = jax.lax.broadcasted_iota(jnp.int32, (DI, E), 1)
    diagonal = jnp.where(row_ids == col_ids, 2.0, 0.0).astype(jnp.float32)
    return (diagonal + noise).astype(jnp.bfloat16)


def setup_inputs(seed: int = 0, part: int = 0) -> dict:
    keys = jax.random.split(jax.random.key(seed), 5)
    part_keys = jax.random.split(jax.random.fold_in(keys[4], part), 5)
    image_features = draw_image_features(jax.random.fold_in(jax.random.fold_in(keys[4], part), 71), part)
    text_embed = draw_text_embed(jax.random.fold_in(jax.random.fold_in(keys[4], part), 71), part)
    image_head = draw_image_head(jax.random.fold_in(jax.random.fold_in(keys[4], part), 71), part)
    logit_scale = jnp.clip(jnp.exp(jax.random.uniform(keys[3], (1,), jnp.float32, math.log(10.0), math.log(40.0))), 10.0, 40.0)
    return dict(image_features=image_features, text_embed=text_embed, image_head=image_head, logit_scale=logit_scale)


def unit_rows(embedding):
    inv_norm = lax.rsqrt(lax.optimization_barrier(jnp.sum(embedding * embedding, axis=1, keepdims=True)) + 1e-06)
    return (embedding * inv_norm, inv_norm)

def norm_backward(embedding, inv_norm, upstream):
    inner = lax.optimization_barrier(jnp.sum(embedding * upstream, axis=1, keepdims=True))
    return (inv_norm * upstream - embedding * (inv_norm * inv_norm * inv_norm) * inner).astype(jnp.bfloat16)

def reference(image_features, text_embed, image_head, logit_scale):
    logit_mult = logit_scale[0]
    img_emb = jnp.dot(image_features, image_head, preferred_element_type=jnp.float32)
    img_scaled, img_inv = unit_rows(img_emb)
    img_unit = img_scaled.astype(jnp.bfloat16)
    txt_emb = text_embed.astype(jnp.float32)
    txt_scaled, txt_inv = unit_rows(txt_emb)
    txt_unit = txt_scaled.astype(jnp.bfloat16)
    logits = logit_mult * jnp.dot(img_unit, txt_unit.T, preferred_element_type=jnp.float32)
    row_lse = jnp.log(lax.optimization_barrier(jnp.sum(jnp.exp(logits), axis=1)))
    col_lse = jnp.log(lax.optimization_barrier(jnp.sum(jnp.exp(logits), axis=0)))
    eye_matrix = jnp.eye(logits.shape[0], dtype=jnp.float32)
    pair_weights = (jnp.exp(logits - row_lse[:, None]) + jnp.exp(logits - col_lse[None, :]) - 2.0 * eye_matrix).astype(jnp.bfloat16)
    img_unit_grad = logit_mult * jnp.dot(pair_weights, txt_unit, preferred_element_type=jnp.float32)
    txt_unit_grad = logit_mult * jnp.dot(pair_weights.T, img_unit, preferred_element_type=jnp.float32)
    img_emb_grad = norm_backward(img_emb, img_inv, img_unit_grad)
    text_embed_grad = norm_backward(txt_emb, txt_inv, txt_unit_grad)
    image_features_grad = jnp.dot(img_emb_grad, image_head.T, preferred_element_type=jnp.float32).astype(jnp.bfloat16)
    feats_blocks = image_features.reshape(N_DP, -1, DI).astype(jnp.float32)
    grad_blocks = img_emb_grad.reshape(N_DP, -1, E).astype(jnp.float32)
    partials = jnp.einsum('kbi,kbe->kie', feats_blocks, grad_blocks)
    partials = lax.optimization_barrier(partials.astype(jnp.bfloat16)).astype(jnp.float32)
    image_head_grad = lax.optimization_barrier(jnp.sum(partials, axis=0))
    return (image_features_grad, text_embed_grad, image_head_grad)
```

```python
import jax
import jax.numpy as jnp
from jax import lax
from jax.sharding import Mesh
from jax.sharding import PartitionSpec as P

NY, NZ = 8, 4
Y, Z = "dp_0", "dp_1"
DP = (Y, Z)


def to_all(array, axis, devices):
    copies = jnp.broadcast_to(array[None], (devices, *array.shape))
    return lax.all_to_all(copies, axis, 0, 0, tiled=True)


def inv_norm(embedding):
    return lax.rsqrt(jnp.sum(embedding * embedding, axis=1, keepdims=True) + 1e-06)


def norm_backward(embedding, inv, upstream):
    inner = jnp.sum(embedding * upstream, axis=1, keepdims=True)
    return (inv * upstream - embedding * (inv * inv * inv) * inner).astype(jnp.bfloat16)


def own_and_sent(partial, received, own, devices):
    rows = partial.shape[0] // devices
    mine = lax.dynamic_slice_in_dim(partial, own * rows, rows, 0)
    ids = jnp.arange(devices, dtype=jnp.int32)[:, None, None]
    others = jnp.where(ids == own, 0.0, received.astype(jnp.float32))
    return jnp.sum(others, axis=0) + mine


def local(image_features, text_embed, image_head, logit_scale):
    scale = logit_scale[0]
    rows = image_features.shape[0]
    a, b = lax.axis_index(Y), lax.axis_index(Z)

    head_parts = to_all(image_head, DP, NY * NZ)
    head = head_parts.reshape(-1, head_parts.shape[-1])

    txt_emb = text_embed.astype(jnp.float32)
    txt_inv = inv_norm(txt_emb)
    txt_unit = (txt_emb * txt_inv).astype(jnp.bfloat16)
    texts = to_all(txt_unit, Y, NY).reshape(NY * rows, -1)

    img_emb = jnp.dot(image_features, head, preferred_element_type=jnp.float32)
    img_inv = inv_norm(img_emb)
    img_unit = (img_emb * img_inv).astype(jnp.bfloat16)
    images = to_all(img_unit, Z, NZ).reshape(NZ * rows, -1)

    logits = scale * lax.dot_general(
        images, texts, (((1,), (1,)), ((), ())), preferred_element_type=jnp.float32
    )
    exps = jnp.exp(logits)
    row_part = jnp.sum(exps, axis=1)
    col_part = jnp.sum(exps, axis=0)

    wide = jnp.pad(row_part, (0, col_part.shape[0] - row_part.shape[0]))
    same_col = (jnp.arange(NZ, dtype=jnp.int32) == b)[None, :, None]
    same_row = (jnp.arange(NY, dtype=jnp.int32) == a)[:, None, None]
    sums = jnp.where(same_col, col_part[None, None, :], jnp.where(same_row, wide[None, None, :], 0.0))
    sums = lax.all_to_all(sums.reshape(NY * NZ, -1), DP, 0, 0, tiled=True).reshape(NY, NZ, -1)
    col_sum = jnp.sum(jnp.where(same_col, sums, 0.0), axis=(0, 1))
    row_sum = jnp.sum(jnp.where(same_row & ~same_col, sums, 0.0), axis=(0, 1))
    row_sum = row_sum[: NZ * rows] + row_part

    i = jnp.arange(NZ * rows, dtype=jnp.int32) - b * rows
    j = jnp.arange(NY * rows, dtype=jnp.int32) - a * rows
    own_i = (i >= 0) & (i < rows)
    label = (i[:, None] == j[None, :]) & own_i[:, None]
    coef = exps * ((1.0 / row_sum)[:, None] + (1.0 / col_sum)[None, :])
    coef = (coef - jnp.where(label, 2.0, 0.0)).astype(jnp.bfloat16)

    img_part = jnp.dot(coef, texts, preferred_element_type=jnp.float32)
    txt_part = lax.dot_general(
        coef, images, (((0,), (0,)), ((), ())), preferred_element_type=jnp.float32
    )
    img_sent = lax.all_to_all(
        img_part.astype(jnp.bfloat16).reshape(NZ, rows, -1), Z, 0, 0, tiled=True
    )
    txt_sent = lax.all_to_all(
        txt_part.astype(jnp.bfloat16).reshape(NY, rows, -1), Y, 0, 0, tiled=True
    )
    img_unit_grad = scale * own_and_sent(img_part, img_sent, b, NZ)
    img_emb_grad = norm_backward(img_emb, img_inv, img_unit_grad)
    head_part = lax.dot_general(
        image_features, img_emb_grad, (((0,), (0,)), ((), ())), preferred_element_type=jnp.float32
    ).astype(jnp.bfloat16)
    head_sent = lax.all_to_all(
        head_part.reshape(NY * NZ, -1, head_part.shape[-1]), DP, 0, 0, tiled=True
    )
    image_features_grad = lax.dot_general(
        img_emb_grad, head, (((1,), (1,)), ((), ())), preferred_element_type=jnp.float32
    ).astype(jnp.bfloat16)
    txt_unit_grad = scale * own_and_sent(txt_part, txt_sent, a, NY)
    text_embed_grad = norm_backward(txt_emb, txt_inv, txt_unit_grad)
    image_head_grad = jnp.sum(head_sent.astype(jnp.float32), axis=0)
    return (image_features_grad, text_embed_grad, image_head_grad)


def solution(mesh):
    split = Mesh(mesh.devices.reshape(mesh.shape["rep"], NY, NZ), ("rep", Y, Z))
    spec = P(("rep", Y, Z), None)
    return jax.shard_map(
        local,
        mesh=split,
        in_specs=(spec, spec, spec, P(None)),
        out_specs=(spec, spec, spec),
        check_vma=False,
    )
```

```python
import jax
import jax.numpy as jnp
from jax import lax
from jax.sharding import Mesh
from jax.sharding import PartitionSpec as P

NY, NZ = 8, 4
Y, Z = "dp_0", "dp_1"


def matmul(left, right, left_dim=1, right_dim=0):
    return lax.dot_general(
        left, right, (((left_dim,), (right_dim,)), ((), ())), preferred_element_type=jnp.float32
    )


def to_all(array):
    copies = jnp.broadcast_to(array[None], (NY, *array.shape))
    return lax.all_to_all(copies, Y, 0, 0, tiled=True)


def shifted(array, distance):
    return lax.ppermute(array, Z, [(k, (k + distance) % NZ) for k in range(NZ)])


def slots_of_all(array):
    return jnp.stack([array] + [shifted(array, k) for k in range(1, NZ)])


def slots_summed(partial):
    sent = partial.astype(jnp.bfloat16)
    others = [shifted(sent[k], -k).astype(jnp.float32) for k in range(1, NZ)]
    return partial[0] + others[0] + others[1] + others[2]


def inv_norm(embedding):
    return lax.rsqrt(jnp.sum(embedding * embedding, axis=1, keepdims=True) + 1e-06)


def norm_backward(embedding, inv, upstream):
    inner = jnp.sum(embedding * upstream, axis=1, keepdims=True)
    return (inv * upstream - embedding * (inv * inv * inv) * inner).astype(jnp.bfloat16)


def column_choice(width, padded, block, b):
    shape = (width, NZ * NY * padded)
    col = lax.broadcasted_iota(jnp.int32, (1, shape[1]), 1)
    slot, rest = col // (NY * padded), col % (NY * padded)
    q, c = rest // padded, rest % padded
    source = (NZ * q + (b + slot) % NZ) * block + c
    source = jnp.where(c < block, source, -1)
    return (lax.broadcasted_iota(jnp.int32, shape, 0) == source).astype(jnp.bfloat16)


def local(image_features, text_embed, image_head, logit_scale):
    scale = logit_scale[0]
    rows, width = image_features.shape
    block, emb_width = image_head.shape
    padded = -(-block // 16) * 16
    a, b = lax.axis_index(Y), lax.axis_index(Z)

    head = to_all(jnp.pad(image_head, ((0, padded - block), (0, 0))))
    head = head.reshape(NY * padded, emb_width)
    choice = column_choice(width, padded, block, b)
    pieces = matmul(image_features, choice).astype(jnp.bfloat16).reshape(rows, NZ, NY * padded)
    features = jnp.stack([pieces[:, 0]] + [shifted(pieces[:, k], k) for k in range(1, NZ)])

    txt_emb = text_embed.astype(jnp.float32)
    txt_inv = inv_norm(txt_emb)
    txt_unit = (txt_emb * txt_inv).astype(jnp.bfloat16)
    txt_unit, head = lax.optimization_barrier((txt_unit, head))
    texts = to_all(txt_unit).reshape(NY * rows, emb_width)

    features = features.reshape(NZ * rows, NY * padded)
    img_emb = slots_summed(matmul(features, head).reshape(NZ, rows, emb_width))
    img_inv = inv_norm(img_emb)
    img_unit = (img_emb * img_inv).astype(jnp.bfloat16)
    images = slots_of_all(img_unit).reshape(NZ * rows, emb_width)

    exps = jnp.exp(scale * matmul(images, texts, 1, 1))
    row_part = jnp.sum(exps, axis=1).reshape(NZ, rows)
    col_part = jnp.sum(exps, axis=0).reshape(NY, rows)
    col_sum = jnp.sum(to_all(col_part), axis=0).reshape(1, NY * rows)
    row_sum = row_part
    for k in range(1, NZ):
        row_sum = row_sum + jnp.roll(shifted(row_part, k), k, axis=0)
    row_sum = row_sum.reshape(NZ * rows, 1)

    i = lax.broadcasted_iota(jnp.int32, exps.shape, 0)
    j = lax.broadcasted_iota(jnp.int32, exps.shape, 1) - a * rows
    label = jnp.where((i == j) & (i < rows), 2.0, 0.0)
    coef = (exps * (1.0 / row_sum + 1.0 / col_sum) - label).astype(jnp.bfloat16)

    img_part = matmul(coef, texts)
    txt_part = matmul(coef, images, 0, 0)
    txt_sent = lax.all_to_all(
        txt_part.astype(jnp.bfloat16).reshape(NY, rows, emb_width), Y, 0, 0, tiled=True
    )
    img_unit_grad = scale * slots_summed(img_part.reshape(NZ, rows, emb_width))
    img_emb_grad = norm_backward(img_emb, img_inv, img_unit_grad)
    grads = slots_of_all(img_emb_grad).reshape(NZ * rows, emb_width)

    head_part = matmul(features, grads, 0, 0).astype(jnp.bfloat16)
    head_part, txt_sent = lax.optimization_barrier((head_part, txt_sent))
    head_sent = lax.all_to_all(
        head_part.reshape(NY, padded, emb_width), Y, 0, 0, tiled=True
    )
    features_part = matmul(grads, head, 1, 1).astype(jnp.bfloat16).reshape(NZ, rows, NY * padded)
    features_part = jnp.concatenate(
        [features_part[0]] + [shifted(features_part[k], -k) for k in range(1, NZ)], axis=1
    )
    image_features_grad = matmul(features_part, choice, 1, 1).astype(jnp.bfloat16)

    mine = lax.dynamic_slice_in_dim(txt_part, a * rows, rows, 0)
    ids = jnp.arange(NY, dtype=jnp.int32)[:, None, None]
    others = jnp.where(ids == a, 0.0, txt_sent.astype(jnp.float32))
    txt_unit_grad = scale * (jnp.sum(others, axis=0) + mine)
    text_embed_grad = norm_backward(txt_emb, txt_inv, txt_unit_grad)
    image_head_grad = jnp.sum(head_sent.astype(jnp.float32), axis=0)[:block]
    return (image_features_grad, text_embed_grad, image_head_grad)


def solution(mesh):
    split = Mesh(mesh.devices.reshape(mesh.shape["rep"], NY, NZ), ("rep", Y, Z))
    spec = P(("rep", Y, Z), None)
    return jax.shard_map(
        local,
        mesh=split,
        in_specs=(spec, spec, spec, P(None)),
        out_specs=(spec, spec, spec),
        check_vma=False,
    )
```

```python
import jax
import jax.numpy as jnp
from jax import lax
from jax.sharding import Mesh
from jax.sharding import PartitionSpec as P

NQ, NP, NZ = 4, 2, 4
NY = NQ * NP
Q, PAIR, Z = "dp_q", "dp_pair", "dp_z"
Y = (Q, PAIR)
SAME = (Q, Z)
DP = (Q, PAIR, Z)


def matmul(left, right, left_dim=1, right_dim=0):
    return lax.dot_general(
        left, right, (((left_dim,), (right_dim,)), ((), ())), preferred_element_type=jnp.float32
    )


def to_all(array, axes, devices):
    copies = jnp.broadcast_to(array[None], (devices, *array.shape))
    return lax.all_to_all(copies, axes, 0, 0, tiled=True)


def swapped(array):
    return lax.ppermute(array, PAIR, [(0, 1), (1, 0)])


def shifted(array, distance):
    return lax.ppermute(array, Z, [(k, (k + distance) % NZ) for k in range(NZ)])


def inv_norm(embedding):
    return lax.rsqrt(jnp.sum(embedding * embedding, axis=1, keepdims=True) + 1e-06)


def norm_backward(embedding, inv, upstream):
    inner = jnp.sum(embedding * upstream, axis=1, keepdims=True)
    return (inv * upstream - embedding * (inv * inv * inv) * inner).astype(jnp.bfloat16)


def column_choice(width, padded, block, p):
    half = NQ * NZ * padded
    shape = (width, NP * half)
    col = lax.broadcasted_iota(jnp.int32, (1, shape[1]), 1)
    slot, place, c = col // half, (col % half) // padded, col % padded
    owner = (place // NZ * NP + (p + slot) % NP) * NZ + place % NZ
    source = jnp.where(c < block, owner * block + c, -1)
    return (lax.broadcasted_iota(jnp.int32, shape, 0) == source).astype(jnp.bfloat16)


def local(image_features, text_embed, image_head, logit_scale):
    scale = logit_scale[0]
    rows, width = image_features.shape
    block, emb_width = image_head.shape
    padded = -(-block // 16) * 16
    half = NQ * NZ * padded
    p, b = lax.axis_index(PAIR), lax.axis_index(Z)
    a = lax.axis_index(Y)

    head = to_all(jnp.pad(image_head, ((0, padded - block), (0, 0))), SAME, NQ * NZ)
    head = head.reshape(half, emb_width)
    choice = column_choice(width, padded, block, p)
    kept = matmul(image_features, choice[:, :half]).astype(jnp.bfloat16)
    given = matmul(image_features, choice[:, half:]).astype(jnp.bfloat16)
    taken = swapped(given)
    partner_part = matmul(taken, head).astype(jnp.bfloat16)

    txt_emb = text_embed.astype(jnp.float32)
    txt_inv = inv_norm(txt_emb)
    txt_unit = (txt_emb * txt_inv).astype(jnp.bfloat16)
    txt_sent, partner_part = lax.optimization_barrier((txt_unit, partner_part))
    texts = to_all(txt_sent, Y, NY).reshape(NY * rows, emb_width)

    img_emb = matmul(kept, head) + swapped(partner_part).astype(jnp.float32)
    img_inv = inv_norm(img_emb)
    img_unit = (img_emb * img_inv).astype(jnp.bfloat16)
    images = lax.all_gather(img_unit, Z, axis=0, tiled=True)

    exps = jnp.exp(scale * matmul(images, texts, 1, 1))
    row_part = jnp.sum(exps, axis=1)
    col_part = jnp.sum(exps, axis=0)

    wide = jnp.pad(row_part, (0, col_part.shape[0] - row_part.shape[0]))
    same_col = (jnp.arange(NZ, dtype=jnp.int32) == b)[None, :, None]
    same_row = (jnp.arange(NY, dtype=jnp.int32) == a)[:, None, None]
    sums = jnp.where(same_col, col_part[None, None, :], jnp.where(same_row, wide[None, None, :], 0.0))
    sums = lax.all_to_all(sums.reshape(NY * NZ, -1), DP, 0, 0, tiled=True).reshape(NY, NZ, -1)
    col_sum = jnp.sum(jnp.where(same_col, sums, 0.0), axis=(0, 1))
    row_sum = jnp.sum(jnp.where(same_row & ~same_col, sums, 0.0), axis=(0, 1))
    row_sum = row_sum[: NZ * rows] + row_part

    i = lax.broadcasted_iota(jnp.int32, exps.shape, 0) - b * rows
    j = lax.broadcasted_iota(jnp.int32, exps.shape, 1) - a * rows
    label = jnp.where((i == j) & (i >= 0) & (i < rows), 2.0, 0.0)
    coef = exps * ((1.0 / row_sum)[:, None] + (1.0 / col_sum)[None, :])
    coef = (coef - label).astype(jnp.bfloat16)

    img_part = matmul(coef, texts)
    txt_part = matmul(coef, images, 0, 0)
    txt_grads = lax.all_to_all(
        txt_part.astype(jnp.bfloat16).reshape(NY, rows, emb_width), Y, 0, 0, tiled=True
    )
    origin = jnp.uint32(0)
    img_sum = lax.dynamic_slice(
        img_part, (b.astype(jnp.uint32) * rows, origin), (rows, emb_width)
    )
    for k in range(1, NZ):
        start = ((b + NZ - k) & (NZ - 1)).astype(jnp.uint32) * rows
        piece = lax.dynamic_slice(img_part, (start, origin), (rows, emb_width))
        img_sum = img_sum + shifted(piece.astype(jnp.bfloat16), -k).astype(jnp.float32)
    img_emb_grad = norm_backward(img_emb, img_inv, scale * img_sum)
    partner_grad = swapped(img_emb_grad)

    head_part = matmul(kept, img_emb_grad, 0, 0) + matmul(taken, partner_grad, 0, 0)
    head_part, txt_grads = lax.optimization_barrier((head_part.astype(jnp.bfloat16), txt_grads))
    head_grads = lax.all_to_all(
        head_part.reshape(NQ * NZ, padded, emb_width), SAME, 0, 0, tiled=True
    )
    kept_grad = matmul(img_emb_grad, head, 1, 1).astype(jnp.bfloat16)
    given_grad = swapped(matmul(partner_grad, head, 1, 1).astype(jnp.bfloat16))
    image_features_grad = (
        matmul(kept_grad, choice[:, :half], 1, 1) + matmul(given_grad, choice[:, half:], 1, 1)
    ).astype(jnp.bfloat16)

    txt_own = lax.dynamic_slice(
        txt_part, (a.astype(jnp.uint32) * rows, origin), (rows, emb_width)
    )
    ids = jnp.arange(NY, dtype=jnp.int32)[:, None, None]
    others = jnp.where(ids == a, 0.0, txt_grads.astype(jnp.float32))
    txt_unit_grad = scale * (jnp.sum(others, axis=0) + txt_own)
    text_embed_grad = norm_backward(txt_emb, txt_inv, txt_unit_grad)
    image_head_grad = jnp.sum(head_grads.astype(jnp.float32), axis=0)[:block]
    return (image_features_grad, text_embed_grad, image_head_grad)


def solution(mesh):
    split = Mesh(mesh.devices.reshape(mesh.shape["rep"], NQ, NP, NZ), ("rep", Q, PAIR, Z))
    spec = P(("rep", Q, PAIR, Z), None)
    return jax.shard_map(
        local,
        mesh=split,
        in_specs=(spec, spec, spec, P(None)),
        out_specs=(spec, spec, spec),
        check_vma=False,
    )
```

```python
import jax
import jax.numpy as jnp
from jax import lax
from jax.sharding import Mesh
from jax.sharding import PartitionSpec as P


NY, NZ = 8, 4
Y, Z = "dp_0", "dp_1"


def matmul(left, right, left_dim=1, right_dim=0):
    return lax.dot_general(
        left, right, (((left_dim,), (right_dim,)), ((), ())), preferred_element_type=jnp.float32
    )


def to_all(array):
    copies = jnp.broadcast_to(array[None], (NY, *array.shape))
    return lax.all_to_all(copies, Y, 0, 0, tiled=True)


def shifted(array, distance):
    return lax.ppermute(array, Z, [(k, (k + distance) % NZ) for k in range(NZ)])


def rows_of(array, index, rows):
    start = index.astype(jnp.uint32) * rows
    return lax.dynamic_slice(array, (start, jnp.uint32(0)), (rows, array.shape[1]))


def inv_norm(embedding):
    return lax.rsqrt(jnp.sum(embedding * embedding, axis=1, keepdims=True) + 1e-06)


def norm_backward(embedding, inv, upstream):
    inner = jnp.sum(embedding * upstream, axis=1, keepdims=True)
    return (inv * upstream - embedding * (inv * inv * inv) * inner).astype(jnp.bfloat16)


def column_choice(width, padded, block, b):
    shape = (width, NZ * NY * padded)
    col = lax.broadcasted_iota(jnp.int32, (1, shape[1]), 1)
    slot, rest = col // (NY * padded), col % (NY * padded)
    q, c = rest // padded, rest % padded
    source = (NZ * q + (b + slot) % NZ) * block + c
    source = jnp.where(c < block, source, -1)
    return (lax.broadcasted_iota(jnp.int32, shape, 0) == source).astype(jnp.bfloat16)


def local(image_features, text_embed, image_head, logit_scale):
    scale = logit_scale[0]
    rows, width = image_features.shape
    block, emb_width = image_head.shape
    padded = -(-block // 16) * 16
    part = NY * padded
    a, b = lax.axis_index(Y), lax.axis_index(Z)
    below = [(b + NZ - k) & (NZ - 1) for k in range(NZ)]

    head = to_all(jnp.pad(image_head, ((0, padded - block), (0, 0)))).reshape(part, emb_width)
    choice = column_choice(width, padded, block, b)
    pieces = matmul(image_features, choice).astype(jnp.bfloat16)
    pieces = [pieces[:, k * part : (k + 1) * part] for k in range(NZ)]
    features = jnp.concatenate([pieces[0]] + [shifted(pieces[k], k) for k in range(1, NZ)])

    txt_emb = text_embed.astype(jnp.float32)
    txt_inv = inv_norm(txt_emb)
    txt_unit = (txt_emb * txt_inv).astype(jnp.bfloat16)
    txt_unit, head = lax.optimization_barrier((txt_unit, head))
    texts = to_all(txt_unit).reshape(NY * rows, emb_width)

    emb_part = matmul(features, head).reshape(NZ, rows, emb_width)
    emb_sent = emb_part.astype(jnp.bfloat16)
    img_emb = emb_part[0]
    for k in range(1, NZ):
        received = shifted(emb_sent[k], -k)
        img_emb = img_emb + received.astype(jnp.float32)
    img_inv = inv_norm(img_emb)
    img_unit = (img_emb * img_inv).astype(jnp.bfloat16)
    images = lax.all_gather(img_unit, Z, axis=0, tiled=True)

    exps = jnp.exp(scale * matmul(images, texts, 1, 1))
    row_part = jnp.sum(exps, axis=1)
    col_part = jnp.sum(exps, axis=0).reshape(NY, rows)
    col_sum = jnp.sum(to_all(col_part), axis=0).reshape(1, NY * rows)
    row_sum = lax.psum(row_part, Z).reshape(NZ * rows, 1)

    i = lax.broadcasted_iota(jnp.int32, exps.shape, 0) - b * rows
    j = lax.broadcasted_iota(jnp.int32, exps.shape, 1) - a * rows
    label = jnp.where((i == j) & (i >= 0) & (i < rows), 2.0, 0.0)
    coef = (exps * (1.0 / row_sum + 1.0 / col_sum) - label).astype(jnp.bfloat16)

    img_part = matmul(coef, texts)
    txt_part = matmul(coef, images, 0, 0)
    txt_grads = lax.all_to_all(
        txt_part.astype(jnp.bfloat16).reshape(NY, rows, emb_width), Y, 0, 0, tiled=True
    )
    img_sum = rows_of(img_part, b, rows)
    for k in range(1, NZ):
        piece = rows_of(img_part, below[k], rows).astype(jnp.bfloat16)
        img_sum = img_sum + shifted(piece, -k).astype(jnp.float32)
    img_emb_grad = norm_backward(img_emb, img_inv, scale * img_sum)
    grads = lax.all_gather(img_emb_grad, Z, axis=0, tiled=True)

    in_order = jnp.concatenate([rows_of(features, (b + NZ - c) & (NZ - 1), rows) for c in range(NZ)])
    head_part = matmul(in_order, grads, 0, 0).astype(jnp.bfloat16)
    head_part, txt_grads = lax.optimization_barrier((head_part, txt_grads))
    head_grads = lax.all_to_all(head_part.reshape(NY, padded, emb_width), Y, 0, 0, tiled=True)
    feat_part = matmul(grads, head, 1, 1).astype(jnp.bfloat16)
    feat_others = [shifted(rows_of(feat_part, below[k], rows), -k) for k in range(1, NZ)]
    feat_part = jnp.concatenate([rows_of(feat_part, b, rows)] + feat_others, axis=1)
    image_features_grad = matmul(feat_part, choice, 1, 1).astype(jnp.bfloat16)

    ids = jnp.arange(NY, dtype=jnp.int32)[:, None, None]
    others = jnp.where(ids == a, 0.0, txt_grads.astype(jnp.float32))
    txt_unit_grad = scale * (jnp.sum(others, axis=0) + rows_of(txt_part, a, rows))
    text_embed_grad = norm_backward(txt_emb, txt_inv, txt_unit_grad)
    image_head_grad = jnp.sum(head_grads.astype(jnp.float32), axis=0)[:block]
    return (image_features_grad, text_embed_grad, image_head_grad)


def solution(mesh):
    split = Mesh(mesh.devices.reshape(mesh.shape["rep"], NY, NZ), ("rep", Y, Z))
    spec = P(("rep", Y, Z), None)

    return jax.shard_map(
        local,
        mesh=split,
        in_specs=(spec, spec, spec, P(None)),
        out_specs=(spec, spec, spec),
        check_vma=False,
    )
```

```python
import jax
import jax.numpy as jnp
from jax import lax
from jax.sharding import Mesh
from jax.sharding import PartitionSpec as P


NQ, NP, NZ = 4, 2, 4
NY = NQ * NP
Q, PAIR, Z = "dp_q", "dp_pair", "dp_z"
Y = (Q, PAIR)
SAME = (Q, Z)


def matmul(left, right, left_dim=1, right_dim=0):
    return lax.dot_general(
        left, right, (((left_dim,), (right_dim,)), ((), ())), preferred_element_type=jnp.float32
    )


def to_all(array, axes, devices):
    copies = jnp.broadcast_to(array[None], (devices, *array.shape))
    return lax.all_to_all(copies, axes, 0, 0, tiled=True)


def swapped(array):
    return lax.ppermute(array, PAIR, [(0, 1), (1, 0)])


def shifted(array, distance):
    return lax.ppermute(array, Z, [(k, (k + distance) % NZ) for k in range(NZ)])


def inv_norm(embedding):
    return lax.rsqrt(jnp.sum(embedding * embedding, axis=1, keepdims=True) + 1e-06)


def norm_backward(embedding, inv, upstream):
    inner = jnp.sum(embedding * upstream, axis=1, keepdims=True)
    return (inv * upstream - embedding * (inv * inv * inv) * inner).astype(jnp.bfloat16)


def column_choice(width, padded, block, p):
    half = NQ * NZ * padded
    shape = (width, NP * half)
    col = lax.broadcasted_iota(jnp.int32, (1, shape[1]), 1)
    slot, place, c = col // half, (col % half) // padded, col % padded
    owner = (place // NZ * NP + (p + slot) % NP) * NZ + place % NZ
    source = jnp.where(c < block, owner * block + c, -1)
    return (lax.broadcasted_iota(jnp.int32, shape, 0) == source).astype(jnp.bfloat16)


def local(image_features, text_embed, image_head, logit_scale):
    scale = logit_scale[0]
    rows, width = image_features.shape
    block, emb_width = image_head.shape
    padded = -(-block // 16) * 16
    half = NQ * NZ * padded
    p, b = lax.axis_index(PAIR), lax.axis_index(Z)
    a = lax.axis_index(Y)

    head = to_all(jnp.pad(image_head, ((0, padded - block), (0, 0))), SAME, NQ * NZ)
    head = head.reshape(half, emb_width)
    choice = column_choice(width, padded, block, p)
    kept = matmul(image_features, choice[:, :half]).astype(jnp.bfloat16)
    given = matmul(image_features, choice[:, half:]).astype(jnp.bfloat16)
    taken = swapped(given)
    partner_part = matmul(taken, head).astype(jnp.bfloat16)

    txt_emb = text_embed.astype(jnp.float32)
    txt_inv = inv_norm(txt_emb)
    txt_unit = (txt_emb * txt_inv).astype(jnp.bfloat16)
    txt_sent, partner_part = lax.optimization_barrier((txt_unit, partner_part))
    texts = to_all(txt_sent, Y, NY).reshape(NY * rows, emb_width)
    returned = swapped(partner_part)

    img_emb = matmul(kept, head) + returned.astype(jnp.float32)
    img_inv = inv_norm(img_emb)
    img_unit = (img_emb * img_inv).astype(jnp.bfloat16)
    images = lax.all_gather(img_unit, Z, axis=0, tiled=True)

    exps = jnp.exp(scale * matmul(images, texts, 1, 1))
    row_part = jnp.sum(exps, axis=1)
    col_part = jnp.sum(exps, axis=0)

    col_sum = jnp.sum(to_all(col_part.reshape(NY, rows), Y, NY), axis=0).reshape(NY * rows)
    row_sum = lax.psum(row_part, Z)

    i = lax.broadcasted_iota(jnp.int32, exps.shape, 0) - b * rows
    j = lax.broadcasted_iota(jnp.int32, exps.shape, 1) - a * rows
    label = jnp.where((i == j) & (i >= 0) & (i < rows), 2.0, 0.0)
    coef = exps * ((1.0 / row_sum)[:, None] + (1.0 / col_sum)[None, :])
    coef = (coef - label).astype(jnp.bfloat16)

    img_part = matmul(coef, texts)
    txt_part = matmul(coef, images, 0, 0)
    txt_grads = lax.all_to_all(
        txt_part.astype(jnp.bfloat16).reshape(NY, rows, emb_width), Y, 0, 0, tiled=True
    )
    origin = jnp.uint32(0)
    img_sum = lax.dynamic_slice(
        img_part, (b.astype(jnp.uint32) * rows, origin), (rows, emb_width)
    )
    for k in range(1, NZ):
        start = ((b + NZ - k) & (NZ - 1)).astype(jnp.uint32) * rows
        piece = lax.dynamic_slice(img_part, (start, origin), (rows, emb_width))
        img_sum = img_sum + shifted(piece.astype(jnp.bfloat16), -k).astype(jnp.float32)
    img_emb_grad = norm_backward(img_emb, img_inv, scale * img_sum)
    partner_grad = swapped(img_emb_grad)

    head_part = matmul(kept, img_emb_grad, 0, 0) + matmul(taken, partner_grad, 0, 0)
    head_part, txt_grads = lax.optimization_barrier((head_part.astype(jnp.bfloat16), txt_grads))
    head_grads = lax.all_to_all(
        head_part.reshape(NQ * NZ, padded, emb_width), SAME, 0, 0, tiled=True
    )
    kept_grad = matmul(img_emb_grad, head, 1, 1).astype(jnp.bfloat16)
    given_grad = swapped(matmul(partner_grad, head, 1, 1).astype(jnp.bfloat16))
    image_features_grad = (
        matmul(kept_grad, choice[:, :half], 1, 1) + matmul(given_grad, choice[:, half:], 1, 1)
    ).astype(jnp.bfloat16)

    txt_own = lax.dynamic_slice(
        txt_part, (a.astype(jnp.uint32) * rows, origin), (rows, emb_width)
    )
    ids = jnp.arange(NY, dtype=jnp.int32)[:, None, None]
    others = jnp.where(ids == a, 0.0, txt_grads.astype(jnp.float32))
    txt_unit_grad = scale * (jnp.sum(others, axis=0) + txt_own)
    text_embed_grad = norm_backward(txt_emb, txt_inv, txt_unit_grad)
    image_head_grad = jnp.sum(head_grads.astype(jnp.float32), axis=0)[:block]
    return (image_features_grad, text_embed_grad, image_head_grad)


def solution(mesh):
    split = Mesh(mesh.devices.reshape(mesh.shape["rep"], NQ, NP, NZ), ("rep", Q, PAIR, Z))
    spec = P(("rep", Q, PAIR, Z), None)

    return jax.shard_map(
        local,
        mesh=split,
        in_specs=(spec, spec, spec, P(None)),
        out_specs=(spec, spec, spec),
        check_vma=False,
    )
```

```python
import jax
import jax.numpy as jnp
from jax import lax
from jax.sharding import Mesh
from jax.sharding import PartitionSpec as P


NQ, NP, NZ = 4, 2, 4
NY = NQ * NP
Q, PAIR, Z = "dp_q", "dp_pair", "dp_z"
Y = (Q, PAIR)
SAME = (Q, Z)


def matmul(left, right, left_dim=1, right_dim=0):
    return lax.dot_general(
        left, right, (((left_dim,), (right_dim,)), ((), ())), preferred_element_type=jnp.float32
    )


def to_all(array, axes, devices):
    copies = jnp.broadcast_to(array[None], (devices, *array.shape))
    return lax.all_to_all(copies, axes, 0, 0, tiled=True)


def swapped(array):
    return lax.ppermute(array, PAIR, [(0, 1), (1, 0)])


def shifted(array, distance):
    return lax.ppermute(array, Z, [(k, (k + distance) % NZ) for k in range(NZ)])


def inv_norm(embedding):
    return lax.rsqrt(jnp.sum(embedding * embedding, axis=1, keepdims=True) + 1e-06)


def norm_backward(embedding, inv, upstream):
    inner = jnp.sum(embedding * upstream, axis=1, keepdims=True)
    return (inv * upstream - embedding * (inv * inv * inv) * inner).astype(jnp.bfloat16)


def column_choice(width, padded, block, p):
    half = NQ * NZ * padded
    shape = (width, NP * half)
    col = lax.broadcasted_iota(jnp.int32, (1, shape[1]), 1)
    slot, place, c = col // half, (col % half) // padded, col % padded
    owner = (place // NZ * NP + (p + slot) % NP) * NZ + place % NZ
    source = jnp.where(c < block, owner * block + c, -1)
    return (lax.broadcasted_iota(jnp.int32, shape, 0) == source).astype(jnp.bfloat16)


def local(image_features, text_embed, image_head, logit_scale):
    scale = logit_scale[0]
    rows, width = image_features.shape
    block, emb_width = image_head.shape
    padded = -(-block // 16) * 16
    half = NQ * NZ * padded
    p, b = lax.axis_index(PAIR), lax.axis_index(Z)
    a = lax.axis_index(Y)

    head = to_all(jnp.pad(image_head, ((0, padded - block), (0, 0))), SAME, NQ * NZ)
    head = head.reshape(half, emb_width)
    choice = column_choice(width, padded, block, p)
    kept = matmul(image_features, choice[:, :half]).astype(jnp.bfloat16)
    given = matmul(image_features, choice[:, half:]).astype(jnp.bfloat16)
    taken = swapped(given)
    partner_part = matmul(taken, head).astype(jnp.bfloat16)

    txt_emb = text_embed.astype(jnp.float32)
    txt_inv = inv_norm(txt_emb)
    txt_unit = (txt_emb * txt_inv).astype(jnp.bfloat16)
    texts = lax.all_gather(txt_unit, Y, axis=0, tiled=True)
    returned = swapped(partner_part)

    img_emb = matmul(kept, head) + returned.astype(jnp.float32)
    img_inv = inv_norm(img_emb)
    img_unit = (img_emb * img_inv).astype(jnp.bfloat16)
    images = lax.all_gather(img_unit, Z, axis=0, tiled=True)

    exps = jnp.exp(scale * matmul(images, texts, 1, 1))
    row_part = jnp.sum(exps, axis=1)
    col_part = jnp.sum(exps, axis=0)

    col_sum = jnp.sum(to_all(col_part.reshape(NY, rows), Y, NY), axis=0).reshape(NY * rows)
    row_sum = lax.psum(row_part, Z)

    i = lax.broadcasted_iota(jnp.int32, exps.shape, 0) - b * rows
    j = lax.broadcasted_iota(jnp.int32, exps.shape, 1) - a * rows
    label = jnp.where((i == j) & (i >= 0) & (i < rows), 2.0, 0.0)
    coef = exps * ((1.0 / row_sum)[:, None] + (1.0 / col_sum)[None, :])
    coef = (coef - label).astype(jnp.bfloat16)

    img_part = matmul(coef, texts)
    txt_part = matmul(coef, images, 0, 0)
    txt_sum = lax.psum_scatter(
        txt_part.astype(jnp.bfloat16), Y, scatter_dimension=0, tiled=True
    )
    origin = jnp.uint32(0)
    img_sum = lax.dynamic_slice(
        img_part, (b.astype(jnp.uint32) * rows, origin), (rows, emb_width)
    )
    for k in range(1, NZ):
        start = ((b + NZ - k) & (NZ - 1)).astype(jnp.uint32) * rows
        piece = lax.dynamic_slice(img_part, (start, origin), (rows, emb_width))
        img_sum = img_sum + shifted(piece.astype(jnp.bfloat16), -k).astype(jnp.float32)
    img_emb_grad = norm_backward(img_emb, img_inv, scale * img_sum)
    partner_grad = swapped(img_emb_grad)

    head_part = matmul(kept, img_emb_grad, 0, 0) + matmul(taken, partner_grad, 0, 0)
    head_grads = lax.all_to_all(
        head_part.astype(jnp.bfloat16).reshape(NQ * NZ, padded, emb_width), SAME, 0, 0, tiled=True
    )
    kept_grad = matmul(img_emb_grad, head, 1, 1).astype(jnp.bfloat16)
    given_grad = swapped(matmul(partner_grad, head, 1, 1).astype(jnp.bfloat16))
    image_features_grad = (
        matmul(kept_grad, choice[:, :half], 1, 1) + matmul(given_grad, choice[:, half:], 1, 1)
    ).astype(jnp.bfloat16)

    txt_unit_grad = scale * txt_sum.astype(jnp.float32)
    text_embed_grad = norm_backward(txt_emb, txt_inv, txt_unit_grad)
    image_head_grad = jnp.sum(head_grads.astype(jnp.float32), axis=0)[:block]
    return (image_features_grad, text_embed_grad, image_head_grad)


def solution(mesh):
    split = Mesh(mesh.devices.reshape(mesh.shape["rep"], NQ, NP, NZ), ("rep", Q, PAIR, Z))
    spec = P(("rep", Q, PAIR, Z), None)

    return jax.shard_map(
        local,
        mesh=split,
        in_specs=(spec, spec, spec, P(None)),
        out_specs=(spec, spec, spec),
        check_vma=False,
    )
```

```python
import jax
import jax.numpy as jnp
from jax import lax
from jax.sharding import Mesh
from jax.sharding import PartitionSpec as P


NQ, NP, NZ = 4, 2, 4
NY = NQ * NP
Q, PAIR, Z = "dp_q", "dp_pair", "dp_z"
Y = (Q, PAIR)
SAME = (Q, Z)


def matmul(left, right, left_dim=1, right_dim=0):
    return lax.dot_general(
        left, right, (((left_dim,), (right_dim,)), ((), ())), preferred_element_type=jnp.float32
    )


def to_all(array, axes, devices):
    copies = jnp.broadcast_to(array[None], (devices, *array.shape))
    return lax.all_to_all(copies, axes, 0, 0, tiled=True)


def swapped(array):
    return lax.ppermute(array, PAIR, [(0, 1), (1, 0)])


def shifted(array, distance):
    return lax.ppermute(array, Z, [(k, (k + distance) % NZ) for k in range(NZ)])


def inv_norm(embedding):
    return lax.rsqrt(jnp.sum(embedding * embedding, axis=1, keepdims=True) + 1e-06)


def norm_backward(embedding, inv, upstream):
    inner = jnp.sum(embedding * upstream, axis=1, keepdims=True)
    return (inv * upstream - embedding * (inv * inv * inv) * inner).astype(jnp.bfloat16)


def column_choice(width, padded, block):
    shape = (width, NP * NQ * NZ * padded)
    col = lax.broadcasted_iota(jnp.int32, (1, shape[1]), 1)
    place, c = col // padded, col % padded
    owner = (place // NZ % NQ * NP + place // (NQ * NZ)) * NZ + place % NZ
    source = jnp.where(c < block, owner * block + c, -1)
    return (lax.broadcasted_iota(jnp.int32, shape, 0) == source).astype(jnp.bfloat16)


def rows_of(array, index, rows):
    start = index.astype(jnp.uint32) * rows
    return lax.dynamic_slice(array, (start, jnp.uint32(0)), (rows, array.shape[1]))


def local(image_features, text_embed, image_head, logit_scale):
    scale = logit_scale[0]
    rows, width = image_features.shape
    block, emb_width = image_head.shape
    padded = -(-block // 16) * 16
    half = NQ * NZ * padded
    p, b = lax.axis_index(PAIR), lax.axis_index(Z)
    a = lax.axis_index(Y)
    below = [(b + NZ - k) & (NZ - 1) for k in range(NZ)]

    head = to_all(jnp.pad(image_head, ((0, padded - block), (0, 0))), SAME, NQ * NZ)
    head = head.reshape(half, emb_width)
    choice = column_choice(width, padded, block)
    own_features = matmul(image_features, choice).astype(jnp.bfloat16)
    first, second = own_features[:, :half], own_features[:, half:]
    kept, given = jnp.where(p == 0, first, second), jnp.where(p == 0, second, first)
    taken = swapped(given)
    features = jnp.concatenate([own_features] + [shifted(own_features, k) for k in range(1, NZ)])
    partner_part = matmul(taken, head).astype(jnp.bfloat16)

    txt_emb = text_embed.astype(jnp.float32)
    txt_inv = inv_norm(txt_emb)
    txt_unit = (txt_emb * txt_inv).astype(jnp.bfloat16)
    texts = lax.all_gather(txt_unit, Y, axis=0, tiled=True)
    returned = swapped(partner_part)
    other_head = swapped(head)

    img_emb = matmul(kept, head) + returned.astype(jnp.float32)
    img_inv = inv_norm(img_emb)
    img_unit = (img_emb * img_inv).astype(jnp.bfloat16)
    images = lax.all_gather(img_unit, Z, axis=0, tiled=True)

    exps = jnp.exp(scale * matmul(images, texts, 1, 1))
    row_part = jnp.sum(exps, axis=1)
    col_part = jnp.sum(exps, axis=0)
    col_parts = to_all(col_part.reshape(NY, rows), Y, NY)
    col_sum = jnp.sum(col_parts, axis=0).reshape(NY * rows)
    own_slot = (jnp.arange(NZ, dtype=jnp.int32) == b)[:, None]
    inv_slots = jnp.where(own_slot, img_inv.reshape(1, rows), 0.0)
    both = lax.psum(jnp.concatenate([row_part, inv_slots.reshape(NZ * rows)]), Z)
    row_sum, inv_all = both[: NZ * rows], both[NZ * rows :].reshape(NZ * rows, 1)

    i = lax.broadcasted_iota(jnp.int32, exps.shape, 0) - b * rows
    j = lax.broadcasted_iota(jnp.int32, exps.shape, 1) - a * rows
    label = jnp.where((i == j) & (i >= 0) & (i < rows), 2.0, 0.0)
    coef = exps * ((1.0 / row_sum)[:, None] + (1.0 / col_sum)[None, :])
    coef = (coef - label).astype(jnp.bfloat16)

    txt_part = matmul(coef, images, 0, 0).astype(jnp.bfloat16)
    coef, txt_part = lax.optimization_barrier((coef, txt_part))
    txt_sum = lax.psum_scatter(txt_part, Y, scatter_dimension=0, tiled=True)

    img_part = scale * matmul(coef, texts)
    units = images.astype(jnp.float32)
    inner = jnp.sum(units * img_part, axis=1, keepdims=True)
    grad_part = (inv_all * (img_part - units * inner)).astype(jnp.bfloat16)
    grad_part = jnp.concatenate([rows_of(grad_part, below[k], rows) for k in range(NZ)])
    head_part = matmul(features, grad_part, 0, 0).astype(jnp.bfloat16)
    head_grads = lax.all_to_all(
        head_part.reshape(NP * NQ * NZ, padded, emb_width), (PAIR, Q, Z), 0, 0, tiled=True
    )

    img_sum = rows_of(img_part, b, rows)
    for k in range(1, NZ):
        piece = rows_of(img_part, below[k], rows).astype(jnp.bfloat16)
        received = shifted(piece, -k)
        img_sum = img_sum + received.astype(jnp.float32)
    img_emb_grad = norm_backward(img_emb, img_inv, img_sum)
    first = matmul(img_emb_grad, jnp.where(p == 0, head, other_head), 1, 1)
    second = matmul(img_emb_grad, jnp.where(p == 0, other_head, head), 1, 1)
    feat_grad = jnp.concatenate([first, second], axis=1).astype(jnp.bfloat16)
    image_features_grad = matmul(feat_grad, choice, 1, 1).astype(jnp.bfloat16)

    text_embed_grad = norm_backward(txt_emb, txt_inv, scale * txt_sum.astype(jnp.float32))
    image_head_grad = jnp.sum(head_grads.astype(jnp.float32), axis=0)[:block]
    return (image_features_grad, text_embed_grad, image_head_grad)


def solution(mesh):
    split = Mesh(mesh.devices.reshape(mesh.shape["rep"], NQ, NP, NZ), ("rep", Q, PAIR, Z))
    spec = P(("rep", Q, PAIR, Z), None)

    return jax.shard_map(
        local,
        mesh=split,
        in_specs=(spec, spec, spec, P(None)),
        out_specs=(spec, spec, spec),
        check_vma=False,
    )
```

```python
import jax
import jax.numpy as jnp
from jax import lax
from jax.experimental import pallas as pl
from jax.experimental.pallas import tpu as pltpu
from jax.sharding import Mesh
from jax.sharding import PartitionSpec as P


NY, NH, NP = 8, 2, 2
NZ = NH * NP
Y, ZH, PAIR = "dp_y", "dp_zh", "dp_pair"
Z = (ZH, PAIR)
SAME = (Y, ZH)


def matmul(left, right, left_dim=1, right_dim=0):
    return lax.dot_general(
        left, right, (((left_dim,), (right_dim,)), ((), ())), preferred_element_type=jnp.float32
    )


def to_all(array, axes, devices):
    copies = jnp.broadcast_to(array[None], (devices, *array.shape))
    return lax.all_to_all(copies, axes, 0, 0, tiled=True)


def swapped(array):
    return lax.ppermute(array, PAIR, [(0, 1), (1, 0)])


def shifted(array, distance):
    return lax.ppermute(array, Z, [(k, (k + distance) % NZ) for k in range(NZ)])


def from_above(array, distance):
    return lax.ppermute(array, Y, [(k, (k - distance) % NY) for k in range(NY)])


def exps_kernel(place, scale, images, *refs):
    pieces, (exps, texts, sums, cols) = refs[:NY], refs[NY:]
    rows = pieces[0].shape[0]
    total = jnp.zeros(sums.shape, jnp.float32)
    for k in range(NY):
        index = (place[0] + k) & (NY - 1)
        at = pl.ds(pl.multiple_of(index * rows, rows), rows)
        product = lax.dot_general(
            images[...], pieces[k][...], (((1,), (1,)), ((), ())), preferred_element_type=jnp.float32
        )
        values = jnp.exp(scale[0] * product)
        exps[:, at] = values
        texts[at, :] = pieces[k][...]
        cols[pl.ds(index, 1), :] = jnp.sum(values, axis=0, keepdims=True)
        total = total + values
    sums[...] = total


def exps_and_sums(place, scale, images, pieces):
    count, width = images.shape
    rows = pieces[0].shape[0]
    smem = pl.BlockSpec(memory_space=pltpu.SMEM)
    vmem = pl.BlockSpec(memory_space=pltpu.VMEM)
    return pl.pallas_call(
        exps_kernel,
        in_specs=[smem, smem] + [vmem] * (1 + NY),
        out_specs=[vmem] * 4,
        out_shape=[
            jax.ShapeDtypeStruct((count, NY * rows), jnp.float32),
            jax.ShapeDtypeStruct((NY * rows, width), jnp.bfloat16),
            jax.ShapeDtypeStruct((count, rows), jnp.float32),
            jax.ShapeDtypeStruct((NY, rows), jnp.float32),
        ],
        name="exps",
    )(place.reshape(1), scale, images, *pieces)


def inv_norm(embedding):
    return lax.rsqrt(jnp.sum(embedding * embedding, axis=1, keepdims=True) + 1e-06)


def norm_backward(embedding, inv, upstream):
    inner = jnp.sum(embedding * upstream, axis=1, keepdims=True)
    return (inv * upstream - embedding * (inv * inv * inv) * inner).astype(jnp.bfloat16)


def column_choice(width, padded, block, p):
    half = NY * NH * padded
    shape = (width, NP * half)
    col = lax.broadcasted_iota(jnp.int32, (1, shape[1]), 1)
    slot, place, c = col // half, (col % half) // padded, col % padded
    owner = place * NP + (p + slot) % NP
    source = jnp.where(c < block, owner * block + c, -1)
    return (lax.broadcasted_iota(jnp.int32, shape, 0) == source).astype(jnp.bfloat16)


def local(image_features, text_embed, image_head, logit_scale):
    scale = logit_scale[0]
    rows, width = image_features.shape
    block, emb_width = image_head.shape
    padded = -(-block // 16) * 16
    half = NY * NH * padded
    p, b = lax.axis_index(PAIR), lax.axis_index(Z)
    a = lax.axis_index(Y)

    head = to_all(jnp.pad(image_head, ((0, padded - block), (0, 0))), SAME, NY * NH)
    head = head.reshape(half, emb_width)
    choice = column_choice(width, padded, block, p)
    kept = matmul(image_features, choice[:, :half]).astype(jnp.bfloat16)
    given = matmul(image_features, choice[:, half:]).astype(jnp.bfloat16)
    taken = swapped(given)
    partner_part = matmul(taken, head).astype(jnp.bfloat16)

    txt_emb = text_embed.astype(jnp.float32)
    txt_inv = inv_norm(txt_emb)
    txt_unit = (txt_emb * txt_inv).astype(jnp.bfloat16)
    pieces = [txt_unit] + [from_above(txt_unit, k) for k in range(1, NY)]
    returned = swapped(partner_part)

    img_emb = matmul(kept, head) + returned.astype(jnp.float32)
    img_inv = inv_norm(img_emb)
    img_unit = (img_emb * img_inv).astype(jnp.bfloat16)
    images = lax.all_gather(img_unit, Z, axis=0, tiled=True)

    exps, texts, row_part, col_part = exps_and_sums(a, logit_scale, images, pieces)
    col_parts = to_all(col_part, Y, NY)
    col_sum = jnp.sum(col_parts, axis=0).reshape(NY * rows)
    row_sum = lax.psum(jnp.sum(row_part, axis=1), Z)

    i = lax.broadcasted_iota(jnp.int32, exps.shape, 0) - b * rows
    j = lax.broadcasted_iota(jnp.int32, exps.shape, 1) - a * rows
    label = jnp.where((i == j) & (i >= 0) & (i < rows), 2.0, 0.0)
    coef = exps * ((1.0 / row_sum)[:, None] + (1.0 / col_sum)[None, :])
    coef = (coef - label).astype(jnp.bfloat16)

    img_part = matmul(coef, texts)
    txt_part = matmul(coef, images, 0, 0)
    txt_grads = lax.all_to_all(
        txt_part.astype(jnp.bfloat16).reshape(NY, rows, emb_width), Y, 0, 0, tiled=True
    )
    origin = jnp.uint32(0)
    img_sum = lax.dynamic_slice(
        img_part, (b.astype(jnp.uint32) * rows, origin), (rows, emb_width)
    )
    for k in range(1, NZ):
        start = ((b + NZ - k) & (NZ - 1)).astype(jnp.uint32) * rows
        piece = lax.dynamic_slice(img_part, (start, origin), (rows, emb_width))
        img_sum = img_sum + shifted(piece.astype(jnp.bfloat16), -k).astype(jnp.float32)
    img_emb_grad = norm_backward(img_emb, img_inv, scale * img_sum)
    partner_grad = swapped(img_emb_grad)

    head_part = matmul(kept, img_emb_grad, 0, 0) + matmul(taken, partner_grad, 0, 0)
    head_part, txt_grads = lax.optimization_barrier((head_part.astype(jnp.bfloat16), txt_grads))
    head_grads = lax.all_to_all(
        head_part.reshape(NY * NH, padded, emb_width), SAME, 0, 0, tiled=True
    )
    kept_grad = matmul(img_emb_grad, head, 1, 1).astype(jnp.bfloat16)
    given_grad = swapped(matmul(partner_grad, head, 1, 1).astype(jnp.bfloat16))
    image_features_grad = (
        matmul(kept_grad, choice[:, :half], 1, 1) + matmul(given_grad, choice[:, half:], 1, 1)
    ).astype(jnp.bfloat16)

    txt_own = lax.dynamic_slice(
        txt_part, (a.astype(jnp.uint32) * rows, origin), (rows, emb_width)
    )
    ids = jnp.arange(NY, dtype=jnp.int32)[:, None, None]
    others = jnp.where(ids == a, 0.0, txt_grads.astype(jnp.float32))
    txt_unit_grad = scale * (jnp.sum(others, axis=0) + txt_own)
    text_embed_grad = norm_backward(txt_emb, txt_inv, txt_unit_grad)
    image_head_grad = jnp.sum(head_grads.astype(jnp.float32), axis=0)[:block]
    return (image_features_grad, text_embed_grad, image_head_grad)


def solution(mesh):
    split = Mesh(mesh.devices.reshape(mesh.shape["rep"], NY, NH, NP), ("rep", Y, ZH, PAIR))
    spec = P(("rep", Y, ZH, PAIR), None)

    return jax.shard_map(
        local,
        mesh=split,
        in_specs=(spec, spec, spec, P(None)),
        out_specs=(spec, spec, spec),
        check_vma=False,
    )
```

```python
import jax
import jax.numpy as jnp
from jax import lax
from jax.sharding import Mesh
from jax.sharding import PartitionSpec as P


NQ, NP, NZ = 4, 2, 4
NY = NQ * NP
Q, PAIR, Z = "dp_q", "dp_pair", "dp_z"
Y = (Q, PAIR)
SAME = (Q, Z)


def matmul(left, right, left_dim=1, right_dim=0):
    return lax.dot_general(
        left, right, (((left_dim,), (right_dim,)), ((), ())), preferred_element_type=jnp.float32
    )


def to_all(array, axes, devices):
    copies = jnp.broadcast_to(array[None], (devices, *array.shape))
    return lax.all_to_all(copies, axes, 0, 0, tiled=True)


def swapped(array):
    return lax.ppermute(array, PAIR, [(0, 1), (1, 0)])


def inv_norm(embedding):
    return lax.rsqrt(jnp.sum(embedding * embedding, axis=1, keepdims=True) + 1e-06)


def norm_backward(embedding, inv, upstream):
    inner = jnp.sum(embedding * upstream, axis=1, keepdims=True)
    return (inv * upstream - embedding * (inv * inv * inv) * inner).astype(jnp.bfloat16)


def column_choice(width, padded, block, p):
    half = NQ * NZ * padded
    shape = (width, NP * half)
    col = lax.broadcasted_iota(jnp.int32, (1, shape[1]), 1)
    slot, place, c = col // half, (col % half) // padded, col % padded
    owner = (place // NZ * NP + (p + slot) % NP) * NZ + place % NZ
    source = jnp.where(c < block, owner * block + c, -1)
    return (lax.broadcasted_iota(jnp.int32, shape, 0) == source).astype(jnp.bfloat16)


def local(image_features, text_embed, image_head, logit_scale):
    scale = logit_scale[0]
    rows, width = image_features.shape
    block, emb_width = image_head.shape
    padded = -(-block // 16) * 16
    half = NQ * NZ * padded
    p, b = lax.axis_index(PAIR), lax.axis_index(Z)
    a = lax.axis_index(Y)

    head = to_all(jnp.pad(image_head, ((0, padded - block), (0, 0))), SAME, NQ * NZ)
    head = head.reshape(half, emb_width)
    choice = column_choice(width, padded, block, p)
    kept = matmul(image_features, choice[:, :half]).astype(jnp.bfloat16)
    given = matmul(image_features, choice[:, half:]).astype(jnp.bfloat16)
    taken = swapped(given)
    partner_part = matmul(taken, head).astype(jnp.bfloat16)

    txt_emb = text_embed.astype(jnp.float32)
    txt_inv = inv_norm(txt_emb)
    txt_unit = (txt_emb * txt_inv).astype(jnp.bfloat16)
    texts = lax.all_gather(txt_unit, Y, axis=0, tiled=True)
    returned = swapped(partner_part)
    other_head = swapped(head)

    img_emb = matmul(kept, head) + returned.astype(jnp.float32)
    img_inv = inv_norm(img_emb)
    img_unit = (img_emb * img_inv).astype(jnp.bfloat16)
    images = lax.all_gather(img_unit, Z, axis=0, tiled=True)

    exps = jnp.exp(scale * matmul(images, texts, 1, 1))
    row_part = jnp.sum(exps, axis=1)
    col_part = jnp.sum(exps, axis=0)

    col_parts = to_all(col_part.reshape(NY, rows), Y, NY)
    col_sum = jnp.sum(col_parts, axis=0).reshape(NY * rows)
    row_sum = lax.psum(row_part, Z)

    i = lax.broadcasted_iota(jnp.int32, exps.shape, 0) - b * rows
    j = lax.broadcasted_iota(jnp.int32, exps.shape, 1) - a * rows
    label = jnp.where((i == j) & (i >= 0) & (i < rows), 2.0, 0.0)
    coef = exps * ((1.0 / row_sum)[:, None] + (1.0 / col_sum)[None, :])
    coef = (coef - label).astype(jnp.bfloat16)

    img_part = matmul(coef, texts)
    txt_part = matmul(coef, images, 0, 0)
    txt_sum = lax.psum_scatter(
        txt_part.astype(jnp.bfloat16), Y, scatter_dimension=0, tiled=True
    )
    origin = jnp.uint32(0)
    img_grads = lax.all_to_all(
        img_part.astype(jnp.bfloat16).reshape(NZ, rows, emb_width), Z, 0, 0, tiled=True
    )
    img_own = lax.dynamic_slice(
        img_part, (b.astype(jnp.uint32) * rows, jnp.uint32(0)), (rows, emb_width)
    )
    ids = jnp.arange(NZ, dtype=jnp.int32)[:, None, None]
    img_sum = img_own + jnp.sum(jnp.where(ids == b, 0.0, img_grads.astype(jnp.float32)), axis=0)
    img_emb_grad = norm_backward(img_emb, img_inv, scale * img_sum)
    partner_grad = swapped(img_emb_grad)

    head_part = matmul(kept, img_emb_grad, 0, 0) + matmul(taken, partner_grad, 0, 0)
    head_grads = lax.all_to_all(
        head_part.astype(jnp.bfloat16).reshape(NQ * NZ, padded, emb_width), SAME, 0, 0, tiled=True
    )
    kept_grad = matmul(img_emb_grad, head, 1, 1).astype(jnp.bfloat16)
    given_grad = matmul(img_emb_grad, other_head, 1, 1).astype(jnp.bfloat16)
    image_features_grad = (
        matmul(kept_grad, choice[:, :half], 1, 1) + matmul(given_grad, choice[:, half:], 1, 1)
    ).astype(jnp.bfloat16)

    txt_unit_grad = scale * txt_sum.astype(jnp.float32)
    text_embed_grad = norm_backward(txt_emb, txt_inv, txt_unit_grad)
    image_head_grad = jnp.sum(head_grads.astype(jnp.float32), axis=0)[:block]
    return (image_features_grad, text_embed_grad, image_head_grad)


def solution(mesh):
    split = Mesh(mesh.devices.reshape(mesh.shape["rep"], NQ, NP, NZ), ("rep", Q, PAIR, Z))
    spec = P(("rep", Q, PAIR, Z), None)

    return jax.shard_map(
        local,
        mesh=split,
        in_specs=(spec, spec, spec, P(None)),
        out_specs=(spec, spec, spec),
        check_vma=False,
    )
```

```python
import jax
import jax.numpy as jnp
from jax import lax
from jax.experimental import pallas as pl
from jax.experimental.pallas import tpu as pltpu
from jax.sharding import Mesh
from jax.sharding import PartitionSpec as P


NQ, NP, NZ = 4, 2, 4
NY = NQ * NP
Q, PAIR, Z = "dp_q", "dp_pair", "dp_z"
Y = (Q, PAIR)
SAME = (Q, Z)


def matmul(left, right, left_dim=1, right_dim=0):
    return lax.dot_general(
        left, right, (((left_dim,), (right_dim,)), ((), ())), preferred_element_type=jnp.float32
    )


def to_all(array, axes, devices):
    copies = jnp.broadcast_to(array[None], (devices, *array.shape))
    return lax.all_to_all(copies, axes, 0, 0, tiled=True)


def swapped(array):
    return lax.ppermute(array, PAIR, [(0, 1), (1, 0)])


def coef_kernel(place, exps, row_inv, col_inv, images, texts, img_sent, img_own, txt_sent, coef, img_part):
    a, b = place[0], place[1]
    rows = img_own.shape[0]
    eye = lax.broadcasted_iota(jnp.int32, (rows, rows), 0) == lax.broadcasted_iota(
        jnp.int32, (rows, rows), 1
    )
    for r in range(NZ):
        at_row = slice(r * rows, (r + 1) * rows)
        inverse = row_inv[at_row, :]
        for c in range(NY):
            at = (at_row, slice(c * rows, (c + 1) * rows))
            label = jnp.where(eye, jnp.where((a == c) & (b == r), 2.0, 0.0), 0.0)
            coef[at] = (exps[at] * (inverse + col_inv[c : c + 1, :]) - label).astype(jnp.bfloat16)
    img_part[...] = jnp.dot(coef[...], texts[...], preferred_element_type=jnp.float32)
    img_sent[...] = img_part[...].astype(jnp.bfloat16)
    img_own[...] = img_part[pl.ds(pl.multiple_of(b * rows, rows), rows), :]
    txt_sent[...] = lax.dot_general(
        coef[...], images[...], (((0,), (0,)), ((), ())), preferred_element_type=jnp.float32
    ).astype(jnp.bfloat16)


def coef_products(place, exps, row_inv, col_inv, images, texts):
    rows = row_inv.shape[1]
    smem = pl.BlockSpec(memory_space=pltpu.SMEM)
    vmem = pl.BlockSpec(memory_space=pltpu.VMEM)
    width = images.shape[1]
    return pl.pallas_call(
        coef_kernel,
        in_specs=[smem] + [vmem] * 5,
        out_specs=[vmem] * 3,
        out_shape=[
            jax.ShapeDtypeStruct(images.shape, jnp.bfloat16),
            jax.ShapeDtypeStruct((rows, width), jnp.float32),
            jax.ShapeDtypeStruct(texts.shape, jnp.bfloat16),
        ],
        scratch_shapes=[
            pltpu.VMEM(exps.shape, jnp.bfloat16),
            pltpu.VMEM(images.shape, jnp.float32),
        ],
        name="coef_products",
    )(place, exps, row_inv, col_inv, images, texts)


def inv_norm(embedding):
    return lax.rsqrt(jnp.sum(embedding * embedding, axis=1, keepdims=True) + 1e-06)


def norm_backward(embedding, inv, upstream):
    inner = jnp.sum(embedding * upstream, axis=1, keepdims=True)
    return (inv * upstream - embedding * (inv * inv * inv) * inner).astype(jnp.bfloat16)


def column_choice(width, padded, block, p):
    half = NQ * NZ * padded
    shape = (width, NP * half)
    col = lax.broadcasted_iota(jnp.int32, (1, shape[1]), 1)
    slot, place, c = col // half, (col % half) // padded, col % padded
    owner = (place // NZ * NP + (p + slot) % NP) * NZ + place % NZ
    source = jnp.where(c < block, owner * block + c, -1)
    return (lax.broadcasted_iota(jnp.int32, shape, 0) == source).astype(jnp.bfloat16)


def local(image_features, text_embed, image_head, logit_scale):
    scale = logit_scale[0]
    rows, width = image_features.shape
    block, emb_width = image_head.shape
    padded = -(-block // 16) * 16
    half = NQ * NZ * padded
    p, b = lax.axis_index(PAIR), lax.axis_index(Z)
    a = lax.axis_index(Y)

    head = to_all(jnp.pad(image_head, ((0, padded - block), (0, 0))), SAME, NQ * NZ)
    head = head.reshape(half, emb_width)
    choice = column_choice(width, padded, block, p)
    own_features = matmul(image_features, choice).astype(jnp.bfloat16)
    kept, given = own_features[:, :half], own_features[:, half:]
    taken = swapped(given)
    partner_part = matmul(taken, head).astype(jnp.bfloat16)

    txt_emb = text_embed.astype(jnp.float32)
    txt_inv = inv_norm(txt_emb)
    txt_unit = (txt_emb * txt_inv).astype(jnp.bfloat16)
    texts = lax.all_gather(txt_unit, Y, axis=0, tiled=True)
    returned = swapped(partner_part)
    other_head = swapped(head)

    img_emb = matmul(kept, head) + returned.astype(jnp.float32)
    img_inv = inv_norm(img_emb)
    img_unit = (img_emb * img_inv).astype(jnp.bfloat16)
    images = lax.all_gather(img_unit, Z, axis=0, tiled=True)

    exps = jnp.exp(scale * matmul(images, texts, 1, 1))
    row_part = jnp.sum(exps, axis=1)
    col_part = jnp.sum(exps, axis=0)

    col_parts = to_all(col_part.reshape(NY, rows), Y, NY)
    col_inv = 1.0 / jnp.sum(col_parts, axis=0)
    row_sum = lax.psum(row_part, Z)
    row_inv = jnp.broadcast_to((1.0 / row_sum)[:, None], (NZ * rows, rows))

    img_sent, img_own, txt_sent = coef_products(
        jnp.stack([a, b]), exps, row_inv, col_inv, images, texts
    )
    txt_sum = lax.psum_scatter(txt_sent, Y, scatter_dimension=0, tiled=True)
    img_grads = lax.all_to_all(img_sent.reshape(NZ, rows, emb_width), Z, 0, 0, tiled=True)
    ids = jnp.arange(NZ, dtype=jnp.int32)[:, None, None]
    img_sum = img_own + jnp.sum(jnp.where(ids == b, 0.0, img_grads.astype(jnp.float32)), axis=0)
    img_emb_grad = norm_backward(img_emb, img_inv, scale * img_sum)
    partner_grad = swapped(img_emb_grad)

    head_part = matmul(kept, img_emb_grad, 0, 0) + matmul(taken, partner_grad, 0, 0)
    head_grads = lax.all_to_all(
        head_part.astype(jnp.bfloat16).reshape(NQ * NZ, padded, emb_width), SAME, 0, 0, tiled=True
    )
    kept_grad = matmul(img_emb_grad, head, 1, 1).astype(jnp.bfloat16)
    given_grad = matmul(img_emb_grad, other_head, 1, 1).astype(jnp.bfloat16)
    feat_grad = jnp.concatenate([kept_grad, given_grad], axis=1)
    image_features_grad = matmul(feat_grad, choice, 1, 1).astype(jnp.bfloat16)

    txt_unit_grad = scale * txt_sum.astype(jnp.float32)
    text_embed_grad = norm_backward(txt_emb, txt_inv, txt_unit_grad)
    image_head_grad = jnp.sum(head_grads.astype(jnp.float32), axis=0)[:block]
    return (image_features_grad, text_embed_grad, image_head_grad)


def solution(mesh):
    split = Mesh(mesh.devices.reshape(mesh.shape["rep"], NQ, NP, NZ), ("rep", Q, PAIR, Z))
    spec = P(("rep", Q, PAIR, Z), None)

    return jax.shard_map(
        local,
        mesh=split,
        in_specs=(spec, spec, spec, P(None)),
        out_specs=(spec, spec, spec),
        check_vma=False,
    )
```

```python
import jax
import jax.numpy as jnp
from jax import lax
from jax.experimental import pallas as pl
from jax.experimental.pallas import tpu as pltpu
from jax.sharding import Mesh
from jax.sharding import PartitionSpec as P


NQ, NP, NZ = 4, 2, 4
NY = NQ * NP
Q, PAIR, Z = "dp_q", "dp_pair", "dp_z"
Y = (Q, PAIR)
SAME = (Q, Z)


def matmul(left, right, left_dim=1, right_dim=0):
    return lax.dot_general(
        left, right, (((left_dim,), (right_dim,)), ((), ())), preferred_element_type=jnp.float32
    )


def swapped(array):
    return lax.ppermute(array, PAIR, [(0, 1), (1, 0)])


def copies_kernel(block, copies):
    height = block.shape[0]
    for k in range(copies.shape[0]):
        copies[k, :height, :] = block[...]
        copies[k, height:, :] = jnp.zeros((copies.shape[1] - height, block.shape[1]), block.dtype)


def padded_copies(block, count, height):
    vmem = pl.BlockSpec(memory_space=pltpu.VMEM)
    return pl.pallas_call(
        copies_kernel,
        in_specs=[vmem],
        out_specs=vmem,
        out_shape=jax.ShapeDtypeStruct((count, height, block.shape[1]), block.dtype),
        name="padded_copies",
    )(block)


def exps_kernel(scale, images, texts, exps, row_part, col_copies, col_part):
    r = pl.program_id(0)
    rows = images.shape[0]
    product = lax.dot_general(
        images[...], texts[...], (((1,), (1,)), ((), ())), preferred_element_type=jnp.float32
    )
    values = jnp.exp(scale[0] * product)
    exps[...] = values

    @pl.when(r == 0)
    def _():
        col_part[...] = jnp.zeros(col_part.shape, jnp.float32)

    total = jnp.zeros((rows, rows), jnp.float32)
    for c in range(NY):
        tile = values[:, c * rows : (c + 1) * rows]
        total = total + tile
        col_part[c : c + 1, :] += jnp.sum(tile, axis=0, keepdims=True)
    row_part[pl.ds(r, 1), :] = jnp.sum(total.T, axis=0, keepdims=True)

    @pl.when(r == NZ - 1)
    def _():
        for k in range(NY):
            col_copies[k] = col_part[...]


def exps_and_sums(scale, images, texts):
    rows, width = images.shape[0] // NZ, images.shape[1]
    return pl.pallas_call(
        exps_kernel,
        grid=(NZ,),
        in_specs=[
            pl.BlockSpec(memory_space=pltpu.SMEM),
            pl.BlockSpec((rows, width), lambda r: (r, 0)),
            pl.BlockSpec(texts.shape, lambda r: (0, 0)),
        ],
        out_specs=[
            pl.BlockSpec((rows, NY * rows), lambda r: (r, 0)),
            pl.BlockSpec((NZ, rows), lambda r: (0, 0)),
            pl.BlockSpec((NY, NY, rows), lambda r: (0, 0, 0)),
        ],
        out_shape=[
            jax.ShapeDtypeStruct((NZ * rows, NY * rows), jnp.float32),
            jax.ShapeDtypeStruct((NZ, rows), jnp.float32),
            jax.ShapeDtypeStruct((NY, NY, rows), jnp.float32),
        ],
        scratch_shapes=[pltpu.VMEM((NY, rows), jnp.float32)],
        name="exps",
    )(scale, images, texts)


def coef_kernel(place, exps, row_sum, col_parts, images, texts, img_sent, img_own, txt_sent, coef, img_part):
    a, b = place[0], place[1]
    rows = img_own.shape[0]
    col_sum = col_parts[0]
    for k in range(1, NY):
        col_sum = col_sum + col_parts[k]
    col_inv = 1.0 / col_sum
    row_inv = 1.0 / row_sum[...]
    eye = lax.broadcasted_iota(jnp.int32, (rows, rows), 0) == lax.broadcasted_iota(
        jnp.int32, (rows, rows), 1
    )
    for r in range(NZ):
        at_row = slice(r * rows, (r + 1) * rows)
        inverse = jnp.broadcast_to(row_inv[r : r + 1, :], (rows, rows)).T
        for c in range(NY):
            at = (at_row, slice(c * rows, (c + 1) * rows))
            label = jnp.where(eye, jnp.where((a == c) & (b == r), 2.0, 0.0), 0.0)
            coef[at] = (exps[at] * (inverse + col_inv[c : c + 1, :]) - label).astype(jnp.bfloat16)
    img_part[...] = jnp.dot(coef[...], texts[...], preferred_element_type=jnp.float32)
    img_sent[...] = img_part[...].astype(jnp.bfloat16)
    img_own[...] = img_part[pl.ds(pl.multiple_of(b * rows, rows), rows), :]
    txt_sent[...] = lax.dot_general(
        coef[...], images[...], (((0,), (0,)), ((), ())), preferred_element_type=jnp.float32
    ).astype(jnp.bfloat16)


def coef_products(place, exps, row_sum, col_parts, images, texts):
    rows = row_sum.shape[1]
    smem = pl.BlockSpec(memory_space=pltpu.SMEM)
    vmem = pl.BlockSpec(memory_space=pltpu.VMEM)
    width = images.shape[1]
    return pl.pallas_call(
        coef_kernel,
        in_specs=[smem] + [vmem] * 5,
        out_specs=[vmem] * 3,
        out_shape=[
            jax.ShapeDtypeStruct(images.shape, jnp.bfloat16),
            jax.ShapeDtypeStruct((rows, width), jnp.float32),
            jax.ShapeDtypeStruct(texts.shape, jnp.bfloat16),
        ],
        scratch_shapes=[
            pltpu.VMEM(exps.shape, jnp.bfloat16),
            pltpu.VMEM(images.shape, jnp.float32),
        ],
        name="coef_products",
    )(place, exps, row_sum, col_parts, images, texts)


def inv_norm(embedding):
    return lax.rsqrt(jnp.sum(embedding * embedding, axis=1, keepdims=True) + 1e-06)


def norm_backward(embedding, inv, upstream):
    inner = jnp.sum(embedding * upstream, axis=1, keepdims=True)
    return (inv * upstream - embedding * (inv * inv * inv) * inner).astype(jnp.bfloat16)


def column_choice(width, padded, block, p):
    half = NQ * NZ * padded
    shape = (width, NP * half)
    col = lax.broadcasted_iota(jnp.int32, (1, shape[1]), 1)
    slot, place, c = col // half, (col % half) // padded, col % padded
    owner = (place // NZ * NP + (p + slot) % NP) * NZ + place % NZ
    source = jnp.where(c < block, owner * block + c, -1)
    return (lax.broadcasted_iota(jnp.int32, shape, 0) == source).astype(jnp.bfloat16)


def local(image_features, text_embed, image_head, logit_scale):
    scale = logit_scale[0]
    rows, width = image_features.shape
    block, emb_width = image_head.shape
    padded = -(-block // 16) * 16
    half = NQ * NZ * padded
    p, b = lax.axis_index(PAIR), lax.axis_index(Z)
    a = lax.axis_index(Y)

    head = lax.all_to_all(padded_copies(image_head, NQ * NZ, padded), SAME, 0, 0, tiled=True)
    head = head.reshape(half, emb_width)
    choice = column_choice(width, padded, block, p)
    own_features = matmul(image_features, choice).astype(jnp.bfloat16)
    kept, given = own_features[:, :half], own_features[:, half:]
    taken = swapped(given)
    partner_part = matmul(taken, head).astype(jnp.bfloat16)

    txt_emb = text_embed.astype(jnp.float32)
    txt_inv = inv_norm(txt_emb)
    txt_unit = (txt_emb * txt_inv).astype(jnp.bfloat16)
    texts = lax.all_gather(txt_unit, Y, axis=0, tiled=True)
    returned = swapped(partner_part)
    other_head = swapped(head)

    img_emb = matmul(kept, head) + returned.astype(jnp.float32)
    img_inv = inv_norm(img_emb)
    img_unit = (img_emb * img_inv).astype(jnp.bfloat16)
    images = lax.all_gather(img_unit, Z, axis=0, tiled=True)

    exps, row_part, col_copies = exps_and_sums(logit_scale, images, texts)
    col_parts = lax.all_to_all(col_copies, Y, 0, 0, tiled=True)
    row_sum = lax.psum(row_part, Z)
    img_sent, img_own, txt_sent = coef_products(
        jnp.stack([a, b]), exps, row_sum, col_parts, images, texts
    )
    txt_sum = lax.psum_scatter(txt_sent, Y, scatter_dimension=0, tiled=True)
    img_grads = lax.all_to_all(img_sent.reshape(NZ, rows, emb_width), Z, 0, 0, tiled=True)
    ids = jnp.arange(NZ, dtype=jnp.int32)[:, None, None]
    img_sum = img_own + jnp.sum(jnp.where(ids == b, 0.0, img_grads.astype(jnp.float32)), axis=0)
    img_emb_grad = norm_backward(img_emb, img_inv, scale * img_sum)
    partner_grad = swapped(img_emb_grad)

    head_part = matmul(kept, img_emb_grad, 0, 0) + matmul(taken, partner_grad, 0, 0)
    head_grads = lax.all_to_all(
        head_part.astype(jnp.bfloat16).reshape(NQ * NZ, padded, emb_width), SAME, 0, 0, tiled=True
    )
    kept_grad = matmul(img_emb_grad, head, 1, 1).astype(jnp.bfloat16)
    given_grad = matmul(img_emb_grad, other_head, 1, 1).astype(jnp.bfloat16)
    feat_grad = jnp.concatenate([kept_grad, given_grad], axis=1)
    image_features_grad = matmul(feat_grad, choice, 1, 1).astype(jnp.bfloat16)

    txt_unit_grad = scale * txt_sum.astype(jnp.float32)
    text_embed_grad = norm_backward(txt_emb, txt_inv, txt_unit_grad)
    image_head_grad = jnp.sum(head_grads.astype(jnp.float32), axis=0)[:block]
    return (image_features_grad, text_embed_grad, image_head_grad)


def solution(mesh):
    split = Mesh(mesh.devices.reshape(mesh.shape["rep"], NQ, NP, NZ), ("rep", Q, PAIR, Z))
    spec = P(("rep", Q, PAIR, Z), None)

    return jax.shard_map(
        local,
        mesh=split,
        in_specs=(spec, spec, spec, P(None)),
        out_specs=(spec, spec, spec),
        check_vma=False,
    )
```

```python
import jax
import jax.numpy as jnp
from jax import lax
from jax.experimental import pallas as pl
from jax.experimental.pallas import tpu as pltpu
from jax.sharding import Mesh
from jax.sharding import PartitionSpec as P


NQ, NP, NZ = 4, 2, 4
NY = NQ * NP
Q, PAIR, Z = "dp_q", "dp_pair", "dp_z"
Y = (Q, PAIR)
SAME = (Q, Z)


def matmul(left, right, left_dim=1, right_dim=0):
    return lax.dot_general(
        left, right, (((left_dim,), (right_dim,)), ((), ())), preferred_element_type=jnp.float32
    )


def to_all(array, axes, devices):
    copies = jnp.broadcast_to(array[None], (devices, *array.shape))
    return lax.all_to_all(copies, axes, 0, 0, tiled=True)


def swapped(array):
    return lax.ppermute(array, PAIR, [(0, 1), (1, 0)])


def coef_kernel(
    at_y, at_z, exps, row_sum, col_parts, images, texts, img_sent, img_own, txt_sent, coef, img_part
):
    a, b = at_y[0], at_z[0]
    rows = img_own.shape[0]
    col_sum = col_parts[0]
    for k in range(1, NY):
        col_sum = col_sum + col_parts[k]
    col_inv = 1.0 / col_sum
    row_inv = 1.0 / row_sum[...]
    eye = lax.broadcasted_iota(jnp.int32, (rows, rows), 0) == lax.broadcasted_iota(
        jnp.int32, (rows, rows), 1
    )
    for r in range(NZ):
        at_row = slice(r * rows, (r + 1) * rows)
        inverse = jnp.broadcast_to(row_inv[r : r + 1, :], (rows, rows)).T
        for c in range(NY):
            at = (at_row, slice(c * rows, (c + 1) * rows))
            label = jnp.where(eye, jnp.where((a == c) & (b == r), 2.0, 0.0), 0.0)
            coef[at] = (exps[at] * (inverse + col_inv[c : c + 1, :]) - label).astype(jnp.bfloat16)
    img_part[...] = jnp.dot(coef[...], texts[...], preferred_element_type=jnp.float32)
    img_sent[...] = img_part[...].astype(jnp.bfloat16)
    img_own[...] = img_part[pl.ds(pl.multiple_of(b * rows, rows), rows), :]
    txt_sent[...] = lax.dot_general(
        coef[...], images[...], (((0,), (0,)), ((), ())), preferred_element_type=jnp.float32
    ).astype(jnp.bfloat16)


def coef_products(at_y, at_z, exps, row_sum, col_parts, images, texts):
    rows = row_sum.shape[1]
    smem = pl.BlockSpec(memory_space=pltpu.SMEM)
    vmem = pl.BlockSpec(memory_space=pltpu.VMEM)
    width = images.shape[1]
    return pl.pallas_call(
        coef_kernel,
        in_specs=[smem] * 2 + [vmem] * 5,
        out_specs=[vmem] * 3,
        out_shape=[
            jax.ShapeDtypeStruct(images.shape, jnp.bfloat16),
            jax.ShapeDtypeStruct((rows, width), jnp.float32),
            jax.ShapeDtypeStruct(texts.shape, jnp.bfloat16),
        ],
        scratch_shapes=[
            pltpu.VMEM(exps.shape, jnp.bfloat16),
            pltpu.VMEM(images.shape, jnp.float32),
        ],
        name="coef_products",
    )(at_y.reshape(1), at_z.reshape(1), exps, row_sum, col_parts, images, texts)


def inv_norm(embedding):
    return lax.rsqrt(jnp.sum(embedding * embedding, axis=1, keepdims=True) + 1e-06)


def norm_backward(embedding, inv, upstream):
    inner = jnp.sum(embedding * upstream, axis=1, keepdims=True)
    return (inv * upstream - embedding * (inv * inv * inv) * inner).astype(jnp.bfloat16)


def column_choice(width, padded, block, p):
    half = NQ * NZ * padded
    shape = (width, NP * half)
    col = lax.broadcasted_iota(jnp.int32, (1, shape[1]), 1)
    slot, place, c = col // half, (col % half) // padded, col % padded
    owner = (place // NZ * NP + (p + slot) % NP) * NZ + place % NZ
    source = jnp.where(c < block, owner * block + c, -1)
    return (lax.broadcasted_iota(jnp.int32, shape, 0) == source).astype(jnp.bfloat16)


def local(image_features, text_embed, image_head, logit_scale):
    scale = logit_scale[0]
    rows, width = image_features.shape
    block, emb_width = image_head.shape
    padded = -(-block // 16) * 16
    half = NQ * NZ * padded
    p, b = lax.axis_index(PAIR), lax.axis_index(Z)
    a = lax.axis_index(Y)

    head = to_all(jnp.pad(image_head, ((0, padded - block), (0, 0))), SAME, NQ * NZ)
    head = head.reshape(half, emb_width)
    choice = column_choice(width, padded, block, p)
    own_features = matmul(image_features, choice).astype(jnp.bfloat16)
    kept, given = own_features[:, :half], own_features[:, half:]
    taken = swapped(given)
    partner_part = matmul(taken, head).astype(jnp.bfloat16)

    txt_emb = text_embed.astype(jnp.float32)
    txt_inv = inv_norm(txt_emb)
    txt_unit = (txt_emb * txt_inv).astype(jnp.bfloat16)
    texts = lax.all_gather(txt_unit, Y, axis=0, tiled=True)
    returned = swapped(partner_part)
    other_head = swapped(head)

    img_emb = matmul(kept, head) + returned.astype(jnp.float32)
    img_inv = inv_norm(img_emb)
    img_unit = (img_emb * img_inv).astype(jnp.bfloat16)
    images = lax.all_gather(img_unit, Z, axis=0, tiled=True)

    exps = jnp.exp(scale * matmul(images, texts, 1, 1))
    row_part = jnp.sum(exps, axis=1)
    col_part = jnp.sum(exps, axis=0)

    col_parts = to_all(col_part.reshape(NY, rows), Y, NY)
    row_sum = lax.optimization_barrier(lax.psum(row_part, Z))
    row_sum = row_sum.reshape(NZ, rows)
    img_sent, img_own, txt_sent = coef_products(
        a, b, exps, row_sum, col_parts, images, texts
    )
    txt_sum = lax.psum_scatter(txt_sent, Y, scatter_dimension=0, tiled=True)
    img_grads = lax.all_to_all(img_sent.reshape(NZ, rows, emb_width), Z, 0, 0, tiled=True)
    ids = jnp.arange(NZ, dtype=jnp.int32)[:, None, None]
    img_sum = img_own + jnp.sum(jnp.where(ids == b, 0.0, img_grads.astype(jnp.float32)), axis=0)
    img_emb_grad = norm_backward(img_emb, img_inv, scale * img_sum)
    partner_grad = swapped(img_emb_grad)

    head_part = matmul(kept, img_emb_grad, 0, 0) + matmul(taken, partner_grad, 0, 0)
    head_grads = lax.all_to_all(
        head_part.astype(jnp.bfloat16).reshape(NQ * NZ, padded, emb_width), SAME, 0, 0, tiled=True
    )
    kept_grad = matmul(img_emb_grad, head, 1, 1).astype(jnp.bfloat16)
    given_grad = matmul(img_emb_grad, other_head, 1, 1).astype(jnp.bfloat16)
    feat_grad = jnp.concatenate([kept_grad, given_grad], axis=1)
    image_features_grad = matmul(feat_grad, choice, 1, 1).astype(jnp.bfloat16)

    txt_unit_grad = scale * txt_sum.astype(jnp.float32)
    text_embed_grad = norm_backward(txt_emb, txt_inv, txt_unit_grad)
    image_head_grad = jnp.sum(head_grads.astype(jnp.float32), axis=0)[:block]
    return (image_features_grad, text_embed_grad, image_head_grad)


def solution(mesh):
    split = Mesh(mesh.devices.reshape(mesh.shape["rep"], NQ, NP, NZ), ("rep", Q, PAIR, Z))
    spec = P(("rep", Q, PAIR, Z), None)

    return jax.shard_map(
        local,
        mesh=split,
        in_specs=(spec, spec, spec, P(None)),
        out_specs=(spec, spec, spec),
        check_vma=False,
    )
```

```python
import jax
import jax.numpy as jnp
from jax import lax
from jax.experimental import pallas as pl
from jax.experimental.pallas import tpu as pltpu
from jax.sharding import Mesh
from jax.sharding import PartitionSpec as P


NQ, NP, NZ = 4, 2, 4
NY = NQ * NP
Q, PAIR, Z = "dp_q", "dp_pair", "dp_z"
Y = (Q, PAIR)
SAME = (Q, Z)


def matmul(left, right, left_dim=1, right_dim=0):
    return lax.dot_general(
        left, right, (((left_dim,), (right_dim,)), ((), ())), preferred_element_type=jnp.float32
    )


def to_all(array, axes, devices):
    copies = jnp.broadcast_to(array[None], (devices, *array.shape))
    return lax.all_to_all(copies, axes, 0, 0, tiled=True)


def swapped(array):
    return lax.ppermute(array, PAIR, [(0, 1), (1, 0)])


def coef_kernel(
    at_y, at_z, exps, row_sum, col_parts, images, texts, img_sent, img_own, txt_sent, coef, img_part
):
    a, b = at_y[0], at_z[0]
    rows = img_own.shape[0]
    col_sum = col_parts[0]
    for k in range(1, NY):
        col_sum = col_sum + col_parts[k]
    col_inv = 1.0 / col_sum
    row_inv = 1.0 / row_sum[...]
    eye = lax.broadcasted_iota(jnp.int32, (rows, rows), 0) == lax.broadcasted_iota(
        jnp.int32, (rows, rows), 1
    )
    for r in range(NZ):
        at_row = slice(r * rows, (r + 1) * rows)
        inverse = jnp.broadcast_to(row_inv[r : r + 1, :], (rows, rows)).T
        for c in range(NY):
            at = (at_row, slice(c * rows, (c + 1) * rows))
            label = jnp.where(eye, jnp.where((a == c) & (b == r), 2.0, 0.0), 0.0)
            coef[at] = (exps[at] * (inverse + col_inv[c : c + 1, :]) - label).astype(jnp.bfloat16)
    img_part[...] = jnp.dot(coef[...], texts[...], preferred_element_type=jnp.float32)
    img_sent[...] = img_part[...].astype(jnp.bfloat16)
    img_own[...] = img_part[pl.ds(pl.multiple_of(b * rows, rows), rows), :]
    txt_sent[...] = lax.dot_general(
        coef[...], images[...], (((0,), (0,)), ((), ())), preferred_element_type=jnp.float32
    ).astype(jnp.bfloat16)


def coef_products(at_y, at_z, exps, row_sum, col_parts, images, texts):
    rows = row_sum.shape[1]
    smem = pl.BlockSpec(memory_space=pltpu.SMEM)
    vmem = pl.BlockSpec(memory_space=pltpu.VMEM)
    width = images.shape[1]
    return pl.pallas_call(
        coef_kernel,
        in_specs=[smem] * 2 + [vmem] * 5,
        out_specs=[vmem] * 3,
        out_shape=[
            jax.ShapeDtypeStruct(images.shape, jnp.bfloat16),
            jax.ShapeDtypeStruct((rows, width), jnp.float32),
            jax.ShapeDtypeStruct(texts.shape, jnp.bfloat16),
        ],
        scratch_shapes=[
            pltpu.VMEM(exps.shape, jnp.bfloat16),
            pltpu.VMEM(images.shape, jnp.float32),
        ],
        name="coef_products",
    )(at_y.reshape(1), at_z.reshape(1), exps, row_sum, col_parts, images, texts)


def inv_norm(embedding):
    return lax.rsqrt(jnp.sum(embedding * embedding, axis=1, keepdims=True) + 1e-06)


def norm_backward(embedding, inv, upstream):
    inner = jnp.sum(embedding * upstream, axis=1, keepdims=True)
    return (inv * upstream - embedding * (inv * inv * inv) * inner).astype(jnp.bfloat16)


def column_choice(width, padded, block, p):
    half = NQ * NZ * padded
    shape = (width, NP * half)
    col = lax.broadcasted_iota(jnp.int32, (1, shape[1]), 1)
    slot, place, c = col // half, (col % half) // padded, col % padded
    owner = (place // NZ * NP + (p + slot) % NP) * NZ + place % NZ
    source = jnp.where(c < block, owner * block + c, -1)
    return (lax.broadcasted_iota(jnp.int32, shape, 0) == source).astype(jnp.bfloat16)


def local(image_features, text_embed, image_head, logit_scale):
    scale = logit_scale[0]
    rows, width = image_features.shape
    block, emb_width = image_head.shape
    padded = -(-block // 16) * 16
    half = NQ * NZ * padded
    p, b = lax.axis_index(PAIR), lax.axis_index(Z)
    a = lax.axis_index(Y)

    head = to_all(jnp.pad(image_head, ((0, padded - block), (0, 0))), SAME, NQ * NZ)
    head = head.reshape(half, emb_width)
    choice = column_choice(width, padded, block, p)
    own_features = matmul(image_features, choice).astype(jnp.bfloat16)
    kept, given = own_features[:, :half], own_features[:, half:]
    taken = swapped(given)
    partner_part = matmul(taken, head).astype(jnp.bfloat16)

    txt_emb = text_embed.astype(jnp.float32)
    txt_inv = inv_norm(txt_emb)
    txt_unit = (txt_emb * txt_inv).astype(jnp.bfloat16)
    texts = lax.all_gather(txt_unit, Y, axis=0, tiled=True)
    returned = swapped(partner_part)

    img_emb = matmul(kept, head) + returned.astype(jnp.float32)
    img_inv = inv_norm(img_emb)
    img_unit = (img_emb * img_inv).astype(jnp.bfloat16)
    images = lax.all_gather(img_unit, Z, axis=0, tiled=True)

    exps = jnp.exp(scale * matmul(images, texts, 1, 1))
    row_part = jnp.sum(exps, axis=1)
    col_part = jnp.sum(exps, axis=0)

    col_parts = to_all(col_part.reshape(NY, rows), Y, NY)
    row_sum = lax.psum(row_part.reshape(NZ, rows), Z)
    img_sent, img_own, txt_sent = coef_products(
        a, b, exps, row_sum, col_parts, images, texts
    )
    txt_sum = lax.psum_scatter(txt_sent, Y, scatter_dimension=0, tiled=True)
    img_grads = lax.all_to_all(img_sent.reshape(NZ, rows, emb_width), Z, 0, 0, tiled=True)
    ids = jnp.arange(NZ, dtype=jnp.int32)[:, None, None]
    img_sum = img_own + jnp.sum(jnp.where(ids == b, 0.0, img_grads.astype(jnp.float32)), axis=0)
    img_emb_grad = norm_backward(img_emb, img_inv, scale * img_sum)
    partner_grad = swapped(img_emb_grad)

    head_part = matmul(kept, img_emb_grad, 0, 0) + matmul(taken, partner_grad, 0, 0)
    head_grads = lax.all_to_all(
        head_part.astype(jnp.bfloat16).reshape(NQ * NZ, padded, emb_width), SAME, 0, 0, tiled=True
    )
    kept_grad = matmul(img_emb_grad, head, 1, 1).astype(jnp.bfloat16)
    given_grad = swapped(matmul(partner_grad, head, 1, 1).astype(jnp.bfloat16))
    feat_grad = jnp.concatenate([kept_grad, given_grad], axis=1)
    image_features_grad = matmul(feat_grad, choice, 1, 1).astype(jnp.bfloat16)

    txt_unit_grad = scale * txt_sum.astype(jnp.float32)
    text_embed_grad = norm_backward(txt_emb, txt_inv, txt_unit_grad)
    image_head_grad = jnp.sum(head_grads.astype(jnp.float32), axis=0)[:block]
    return (image_features_grad, text_embed_grad, image_head_grad)


def solution(mesh):
    split = Mesh(mesh.devices.reshape(mesh.shape["rep"], NQ, NP, NZ), ("rep", Q, PAIR, Z))
    spec = P(("rep", Q, PAIR, Z), None)

    return jax.shard_map(
        local,
        mesh=split,
        in_specs=(spec, spec, spec, P(None)),
        out_specs=(spec, spec, spec),
        check_vma=False,
    )
```
